512 devices in a mesh: tm: 8 (over z_hi, core), height: 8 (over x, z_lo), head: 8 (over y).
Axes of the slice: x: 4, y: 8, z: 8 (z_hi: 4, z_lo: 2; z = z_hi * 2 + z_lo), core: 2. Of those that a mesh axis runs over, the one named last changes fastest.
Arguments:
- lat_q: bfloat16 [8, 8, 2, 384, 3072], P('tm', 'height', None, None, 'head'), may hold values from -12 to 12
- lat_kv: bfloat16 [2, 8, 8, 2, 384, 3072], P(None, 'tm', 'height', None, None, 'head'), may hold values from -6 to 6
- txt_qkv: bfloat16 [3, 64, 128, 3072], P(None, ('tm', 'height'), None, 'head'), may hold values from -12 to 12
- blocks: int32 [8, 8, 2, 9], P('tm', 'height'), may hold values from -1 to 127, as said below
- owner: int32 [8], P('head'), may hold values from 0 to 63
Outputs:
- latent_out: bfloat16 [8, 8, 2, 384, 3072], P('tm', 'height', None, None, 'head')
- text_out: bfloat16 [128, 3072], P(None, 'head')
The draws below stay inside these ranges and needn't reach their ends.
Inputs may be any that keep to these rules, and one draw needn't show every extreme that they name: `blocks`: row i lists its own tile i first, then distinct tiles with the same width index whose frame and height tile indices each differ from tile i's by at most one, then -1 entries; some row lists 9 tiles.
All inputs are finite; a program needn't handle non-finite values.
Results may differ from the reference program's by a relative error of at most 0.0031.
Values may be sent and summed in bfloat16 or wider, within the bound.
No kernel may reach another device: no remote copies, remote signals or barrier semaphores. Data moves between devices by JAX's collectives and lax.ppermute only.
A program may use at most 128 MiB of HBM per device.

```python
import jax
import jax.numpy as jnp
from jax import lax

HEADS = 24
HD = 128
TXT = 128
WT = 2
NB = 9
TILE = 384
NTT = 8
NHT = 8
SLOTS = 64
GROUPS = 8


def attention_draw(key, dims_all, query_scale):
    splits = jax.random.split(key, 3)
    queries = jnp.clip(jax.random.normal(splits[0], dims_all, jnp.float32) * query_scale, -12.0, 12.0)
    key_draw = jnp.clip(jax.random.normal(splits[1], dims_all, jnp.float32), -6.0, 6.0)
    value_draw = jnp.clip(jax.random.normal(splits[2], dims_all, jnp.float32), -6.0, 6.0)
    return (queries, key_draw, value_draw)


def draw_lat_q(key, part):
    queries, key_draw, value_draw = attention_draw(jax.random.fold_in(key, 11), (NTT, NHT, WT, TILE, HEADS * HD), 2.5)
    return queries.astype(jnp.bfloat16)


def draw_lat_kv(key, part):
    queries, key_draw, value_draw = attention_draw(jax.random.fold_in(key, 11), (NTT, NHT, WT, TILE, HEADS * HD), 2.5)
    return jnp.stack([key_draw, value_draw]).astype(jnp.bfloat16)


def draw_txt_qkv(key, part):
    queries, key_draw, value_draw = attention_draw(jax.random.fold_in(key, 13), (SLOTS, TXT, HEADS * HD), 3.0)
    return jnp.stack([queries, key_draw, value_draw]).astype(jnp.bfloat16)


def draw_blocks(key, part):
    dims_all = (NTT, NHT, WT, NB)
    time_step = jnp.array([0, -1, -1, -1, 0, 0, 1, 1, 1], jnp.int32)
    height_step = jnp.array([0, -1, 0, 1, -1, 1, -1, 0, 1], jnp.int32)
    tile_time = lax.broadcasted_iota(jnp.int32, dims_all, 0)
    tile_height = lax.broadcasted_iota(jnp.int32, dims_all, 1)
    tile_width = lax.broadcasted_iota(jnp.int32, dims_all, 2)
    entry_slot = lax.broadcasted_iota(jnp.int32, dims_all, 3)
    key_time = tile_time + time_step
    key_height = tile_height + height_step
    inside = (key_time >= 0) & (key_time < NTT) & (key_height >= 0) & (key_height < NHT)
    kept = jax.random.randint(jax.random.fold_in(key, 17), dims_all, 0, 4) > 0
    forced = (tile_time == 1) & (tile_height == 1) & (tile_width == 0)
    listed = inside & (kept | (entry_slot == 0) | forced)
    global_id = (key_time * NHT + key_height) * WT + tile_width
    ordering = jnp.where(listed, 0, 16) + entry_slot
    order_index = jnp.argsort(ordering, axis=-1, stable=True)
    return jnp.take_along_axis(jnp.where(listed, global_id, -1), order_index, axis=-1).astype(jnp.int32)


def with_ends(entries, own_key, low, top_value):
    longest = entries.shape.index(max(entries.shape))
    spots = []
    for shift in (0, 1):
        where = [jax.random.randint(jax.random.fold_in(own_key, axis), (), 0, length) for axis, length in enumerate(entries.shape)]
        where[longest] = (where[longest] + shift) % entries.shape[longest]
        spots.append(tuple(where))
    return entries.at[spots[0]].set(low).at[spots[1]].set(top_value)


def setup_inputs(seed: int = 0) -> dict:
    key_of = jax.random.split(jax.random.key(seed), 6)
    lat_q = draw_lat_q(jax.random.fold_in(key_of[5], 71), 0)
    lat_kv = draw_lat_kv(jax.random.fold_in(key_of[5], 71), 0)
    txt_qkv = draw_txt_qkv(jax.random.fold_in(key_of[5], 71), 0)
    blocks = draw_blocks(jax.random.fold_in(key_of[5], 71), 0)
    owner = with_ends(jax.random.randint(key_of[4], (GROUPS,), 0, SLOTS), jax.random.fold_in(key_of[4], 1), 0, SLOTS - 1).astype(jnp.int32)
    return dict(lat_q=lat_q, lat_kv=lat_kv, txt_qkv=txt_qkv, blocks=blocks, owner=owner)


def reference(lat_q, lat_kv, txt_qkv, blocks, owner):
    all_columns = HEADS * HD
    inv_root = HD ** -0.5
    column_ids = jnp.arange(all_columns, dtype=jnp.int32)
    source_slot = owner[column_ids // (all_columns // GROUPS)].astype(jnp.int32)
    text_index = jnp.arange(TXT, dtype=jnp.int32)
    selected = txt_qkv[:, source_slot[None, :], text_index[:, None], column_ids[None, :]]
    text_query = selected[0].reshape(TXT, HEADS, HD).astype(jnp.float32)
    text_key = selected[1].reshape(TXT, HEADS, HD)
    text_value = selected[2].reshape(TXT, HEADS, HD)
    tile_count = NTT * NHT * WT
    queries = lat_q.reshape(tile_count, TILE, HEADS, HD)
    key_tiles = lat_kv[0].reshape(tile_count, TILE, HEADS, HD)
    value_tiles = lat_kv[1].reshape(tile_count, TILE, HEADS, HD)
    tile_lists = blocks.reshape(tile_count, NB)

    def latent_tile(index):
        listed = tile_lists[index] >= 0
        clamped = jnp.maximum(tile_lists[index], 0).astype(jnp.int32)
        key_rows = jnp.concatenate([key_tiles[clamped].reshape(NB * TILE, HEADS, HD), text_key], 0)
        value_rows = jnp.concatenate([value_tiles[clamped].reshape(NB * TILE, HEADS, HD), text_value], 0)
        key_live = jnp.concatenate([jnp.repeat(listed, TILE), jnp.ones((TXT,), dtype=bool)])
        scores = jnp.einsum("qhd,khd->hqk", queries[index].astype(jnp.float32), key_rows.astype(jnp.float32)) * inv_root
        scores = jnp.where(key_live[None, None, :], scores, jnp.float32(-1e30))
        row_max = jnp.max(scores, axis=-1, keepdims=True)
        weights = jnp.exp(scores - row_max)
        row_sum = jnp.sum(weights, axis=-1)
        rounded = lax.optimization_barrier(weights.astype(jnp.bfloat16))
        mixed = jnp.einsum("hqk,khd->qhd", rounded.astype(jnp.float32), value_rows.astype(jnp.float32))
        mixed = mixed / jnp.transpose(row_sum)[:, :, None]
        return mixed.reshape(TILE, all_columns).astype(jnp.bfloat16)

    latent_out = lax.map(latent_tile, jnp.arange(tile_count, dtype=jnp.int32)).reshape(lat_q.shape)

    def absorb(carry, pieces):
        run_max, run_sum, run_acc = carry
        key_block, value_block = pieces
        scores = jnp.einsum("qhd,khd->hqk", text_query, key_block.astype(jnp.float32)) * inv_root
        new_max = jnp.maximum(run_max, jnp.max(scores, axis=-1))
        weights = jnp.exp(scores - new_max[:, :, None])
        factor = jnp.exp(run_max - new_max)
        run_sum = run_sum * factor + jnp.sum(weights, axis=-1)
        run_acc = run_acc * factor[:, :, None] + jnp.einsum("hqk,khd->hqd", weights, value_block.astype(jnp.float32), precision=lax.Precision.HIGHEST)
        return (new_max, run_sum, run_acc), None

    start = (jnp.full((HEADS, TXT), -1e30, dtype=jnp.float32), jnp.zeros((HEADS, TXT), dtype=jnp.float32), jnp.zeros((HEADS, TXT, HD), dtype=jnp.float32))
    carry, _ = lax.scan(absorb, start, (key_tiles, value_tiles))
    carry, _ = absorb(carry, (text_key, text_value))
    text_mixed = carry[2] / carry[1][:, :, None]
    text_out = jnp.transpose(text_mixed, (1, 0, 2)).reshape(TXT, all_columns).astype(jnp.bfloat16)
    return latent_out, text_out
```

```python
import functools

import jax
import jax.numpy as jnp
from jax import lax
from jax.experimental import pallas as pl
from jax.experimental.pallas import tpu as pltpu
from jax.sharding import Mesh, PartitionSpec as P

HD = 128
LOG2E = 1.4426950408889634
FAR_AWAY = 1e30

AX = ("zh", "core", "x", "zl")
SIZES = (4, 2, 4, 2)
ROWS16 = ("core", "x", "zl")


def flat(place):
    out = 0
    for size, part in zip(SIZES, place):
        out = out * size + part
    return out


def pairs(rule):
    found = []
    for zh in range(SIZES[0]):
        for core in range(SIZES[1]):
            for x in range(SIZES[2]):
                for zl in range(SIZES[3]):
                    target = rule(zh, core, x, zl)
                    if target is None:
                        continue
                    if all(0 <= part < size for part, size in zip(target, SIZES)):
                        found.append((flat((zh, core, x, zl)), flat(target)))
    return found


SWAP_CORE = pairs(lambda zh, c, x, zl: (zh, 1 - c, x, zl))
SWAP_ZL = pairs(lambda zh, c, x, zl: (zh, c, x, 1 - zl))
X_NEAR = pairs(lambda zh, c, x, zl: (zh, c, x - 1 if zl == 0 else x + 1, zl))
X_FAR = pairs(lambda zh, c, x, zl: (zh, c, x + 1 if zl == 0 else x - 1, zl))
NEXT_BLOCK = pairs(lambda zh, c, x, zl: (zh - 1 if zl == 0 else zh + 1, c, x, 1 - zl))
Q_FIRST = pairs(lambda zh, c, x, zl: (zh, 1 - c, x, zl) if c == zl else (zh, c, x, 1 - zl))
Q_SECOND = pairs(lambda zh, c, x, zl: None if c == zl else (zh, 1 - c, x, 1 - zl))
OUT_NEAR = pairs(lambda zh, c, x, zl: None if c == zl else (zh, 1 - c, x, zl))
OUT_FAR_FIRST = pairs(lambda zh, c, x, zl: (zh, c, x, 1 - zl) if c == zl else None)
OUT_FAR_SECOND = pairs(lambda zh, c, x, zl: None if c == zl else (zh, 1 - c, x, 1 - zl))

SCALE = HD ** (-0.5) * LOG2E


def attend(query, keys_values, carry):
    scores = []
    top = None if carry is None else carry[0]
    for keys, _, bias in keys_values:
        score = lax.dot_general(
            query, keys, (((1,), (1,)), ((), ())), preferred_element_type=jnp.float32
        )
        scores.append(score)
        score_top = jnp.max(score, axis=1, keepdims=True)
        if bias is not None:
            score_top = score_top + bias
        top = score_top if top is None else jnp.maximum(top, score_top)
    total = None
    mixed = None
    if carry is not None:
        factor = jnp.exp2((carry[0] - top) * SCALE)
        total = carry[1] * factor
        mixed = carry[2] * factor
    for score, (_, values, bias) in zip(scores, keys_values):
        shift = top if bias is None else top - bias
        weights = jnp.exp2((score - shift) * SCALE)
        part_total = jnp.sum(weights, axis=1, keepdims=True)
        part = jnp.dot(
            weights.astype(jnp.bfloat16), values, preferred_element_type=jnp.float32
        )
        total = part_total if total is None else total + part_total
        mixed = part if mixed is None else mixed + part
    return top, total, mixed


def bias_of(listed_ref, index):
    return jnp.where(listed_ref[index] > 0, 0.0, -FAR_AWAY).astype(jnp.float32)


def pack_stats(top, total, rows):
    lane = lax.broadcasted_iota(jnp.int32, (rows, HD), 1)
    return jnp.where(lane < HD // 2, top, total)


def block_kernel(near_listed, far_listed, near_q, far_q, pair, far_pair, *outs, rows):
    for listed, query, (stats, acc) in (
        (near_listed, near_q, outs[:2]),
        (far_listed, far_q, outs[2:]),
    ):
        tiles = []
        for index, (ref, tile) in enumerate(((pair, 0), (pair, 1), (far_pair, 0), (far_pair, 1))):
            tiles.append((ref[tile, 0], ref[tile, 1], bias_of(listed, index)))
        top, total, mixed = attend(query[...], tiles, None)
        stats[...] = pack_stats(top, total, rows)
        acc[...] = mixed


def rest_kernel(listed, query, two, *refs, singles, rows):
    ones = refs[:singles]
    text, stats, acc, out = refs[singles:]
    tiles = [(text[1], text[2], None)]
    for tile in range(2):
        tiles.append((two[tile, 0], two[tile, 1], bias_of(listed, 4 + tile)))
    for index, ref in enumerate(ones):
        tiles.append((ref[0], ref[1], bias_of(listed, 6 + index)))
    carry = (stats[:, :1], stats[:, HD // 2 : HD // 2 + 1], acc[...])
    _, total, mixed = attend(query[...], tiles, carry)
    out[...] = (mixed / total).astype(jnp.bfloat16)


def column_block(shape):
    zeros = (0,) * (len(shape) - 1)
    return pl.BlockSpec(tuple(shape[:-1]) + (HD,), lambda head: zeros + (head,))


SMEM = pl.BlockSpec(memory_space=pltpu.SMEM)


def block_attention(near_listed, far_listed, near_q, far_q, pair, far_pair):
    rows, columns = pair.shape[2:]
    state = jax.ShapeDtypeStruct((rows, columns), jnp.float32)
    query_spec = pl.BlockSpec((rows, HD), lambda head: (0, head))
    return pl.pallas_call(
        functools.partial(block_kernel, rows=rows),
        grid=(columns // HD,),
        in_specs=[SMEM, SMEM, query_spec, query_spec]
        + [column_block(pair.shape), column_block(far_pair.shape)],
        out_specs=[query_spec] * 4,
        out_shape=[state] * 4,
        name="block_attention",
    )(near_listed, far_listed, near_q, far_q, pair, far_pair)


def rest_attention(listed, query, two, ones, text, stats, acc, name):
    rows, columns = two.shape[2:]
    query_spec = pl.BlockSpec((rows, HD), lambda head: (0, head))
    return pl.pallas_call(
        functools.partial(rest_kernel, singles=len(ones), rows=rows),
        grid=(columns // HD,),
        in_specs=[SMEM, query_spec, column_block(two.shape)]
        + [column_block(one.shape) for one in ones]
        + [column_block(text.shape), query_spec, query_spec],
        out_specs=query_spec,
        out_shape=jax.ShapeDtypeStruct((rows, columns), jnp.bfloat16),
        name=name,
    )(listed, query, two, *ones, text, stats, acc)


def text_kernel(first, text, kv, acc, stats):
    head = pl.program_id(0)
    query = text[0]
    text_bias = bias_of(first, 0)
    parts = [(text[1], text[2], text_bias), (kv[0, 0], kv[1, 0], None), (kv[0, 1], kv[1, 1], None)]
    scores = []
    top = None
    for keys, _, bias in parts:
        score = lax.dot_general(
            query, keys, (((1,), (1,)), ((), ())), preferred_element_type=jnp.float32
        )
        scores.append(score)
        score_top = jnp.max(score, axis=1, keepdims=True)
        if bias is not None:
            score_top = score_top + bias
        top = score_top if top is None else jnp.maximum(top, score_top)
    total = 0.0
    mixed = 0.0
    for score, (_, values, bias) in zip(scores, parts):
        shift = top if bias is None else top - bias
        weights = jnp.exp2((score - shift) * SCALE)
        total = total + jnp.sum(weights, axis=1, keepdims=True)
        high = weights.astype(jnp.bfloat16)
        low = (weights - high.astype(jnp.float32)).astype(jnp.bfloat16)
        mixed = mixed + jnp.dot(high, values, preferred_element_type=jnp.float32)
        mixed = mixed + jnp.dot(low, values, preferred_element_type=jnp.float32)
    acc[0] = mixed
    lane = lax.broadcasted_iota(jnp.int32, stats.shape, 1)
    heads = pl.num_programs(0)

    @pl.when(head == 0)
    def _():
        stats[...] = jnp.zeros(stats.shape, jnp.float32)

    kept = jnp.where(lane == head, top, stats[...])
    stats[...] = jnp.where(lane == head + heads, total, kept)


def text_partial(first, text, kv):
    count, columns = text.shape[1:]
    heads = columns // HD
    return pl.pallas_call(
        text_kernel,
        grid=(heads,),
        in_specs=[SMEM, column_block(text.shape), column_block(kv.shape)],
        out_specs=[
            pl.BlockSpec((1, count, HD), lambda head: (head, 0, 0)),
            pl.BlockSpec((count, HD), lambda head: (0, 0)),
        ],
        out_shape=[
            jax.ShapeDtypeStruct((heads, count, HD), jnp.float32),
            jax.ShapeDtypeStruct((count, HD), jnp.float32),
        ],
        name="text_partial",
    )(first, text, kv)


def merge_kernel(parts, out, *, heads, queries):
    for row in range(queries):
        stats = parts[:, heads * queries + row, :]
        top = jnp.max(stats, axis=0, keepdims=True)
        factor = jnp.exp2((stats - top) * SCALE)
        for head in range(heads):
            weight = factor[:, head : head + 1]
            total = jnp.sum(
                stats[:, heads + head : heads + head + 1] * weight, axis=0, keepdims=True
            )
            mixed = jnp.sum(parts[:, head * queries + row, :] * weight, axis=0, keepdims=True)
            out[row : row + 1, head * HD : (head + 1) * HD] = mixed / total


def merge_text(parts, heads, queries):
    return pl.pallas_call(
        functools.partial(merge_kernel, heads=heads, queries=queries),
        out_shape=jax.ShapeDtypeStruct((queries, heads * HD), jnp.float32),
        name="merge_text",
    )(parts)


def spread(chunk, axis):
    count = lax.axis_size(axis)
    return lax.all_to_all(jnp.broadcast_to(chunk[None], (count,) + chunk.shape), axis, 0, 0)


def owner_text(txt_qkv, owner):
    kinds, _, count, columns = txt_qkv.shape
    group = lax.axis_size(ROWS16)
    pieces = lax.all_to_all(
        txt_qkv.reshape(group, kinds * count // group, columns), ROWS16, 0, 0
    )
    piece = lax.dynamic_index_in_dim(pieces, owner % group, 0, False)
    piece = lax.dynamic_index_in_dim(spread(piece, "zh"), owner // group, 0, False)
    return spread(piece, ROWS16).reshape(kinds, count, columns)


def listed_slots(ids, slots, width):
    found = []
    for frame, height in slots:
        inside = (frame >= 0) & (frame < 8) & (height >= 0) & (height < 8)
        tile = jnp.where(inside, (frame * 8 + height) * 2 + width, -2)
        found.append(tile)
    return jnp.any(jnp.stack(found)[:, None] == ids[None, :], axis=1).astype(jnp.int32)


def body(lat_q, lat_kv, txt_qkv, blocks, owner):
    zh, core, x, zl = (lax.axis_index(axis) for axis in AX)
    rows, columns = lat_q.shape[3:]
    heads = columns // HD
    list_length = blocks.shape[-1]
    queries = lat_q[0, 0]
    kv = lat_kv[:, 0, 0]
    straight = core == zl
    other = jnp.where(straight, 0, 1)

    text = owner_text(txt_qkv, owner[0])

    kept = lax.dynamic_index_in_dim(kv, core, 1, False)
    given = lax.dynamic_index_in_dim(kv, 1 - core, 1, False)
    received = lax.ppermute(given, AX, SWAP_CORE)
    pair = jnp.stack([kept, received])
    far_pair = lax.ppermute(pair, AX, SWAP_ZL)
    x_near = lax.ppermute(pair, AX, X_NEAR)
    b_far = lax.ppermute(lax.dynamic_index_in_dim(pair, other, 0, False), AX, NEXT_BLOCK)

    ids = jnp.pad(
        blocks[0, 0].astype(jnp.bfloat16), ((0, 0), (0, columns - list_length))
    )[:, None, :]
    asked = jnp.concatenate(
        [queries, ids, jnp.zeros((2, 15, columns), jnp.bfloat16)], axis=1
    )
    q_first = lax.ppermute(lax.dynamic_index_in_dim(asked, 1 - zl, 0, False), AX, Q_FIRST)
    q_second = lax.ppermute(lax.dynamic_index_in_dim(asked, zl, 0, False), AX, Q_SECOND)
    own_q = lax.dynamic_index_in_dim(asked, core, 0, False)
    near_q = jnp.where(straight, own_q, q_first)
    far_q = jnp.where(straight, q_first, q_second)

    x_b_far = lax.ppermute(b_far, AX, X_FAR)
    x_far = lax.ppermute(far_pair, AX, X_FAR)
    b_near = lax.ppermute(lax.dynamic_index_in_dim(far_pair, other, 0, False), AX, NEXT_BLOCK)
    x_b_near = lax.ppermute(b_near, AX, X_NEAR)

    first_frame, second_frame = (2 * zh + core, 2 * zh + 1 - core)
    b_frame = jnp.where(zl == 0, 2 * zh - 1, 2 * zh + 2)
    h_near, h_far = (2 * x + zl, 2 * x + 1 - zl)
    h_x_near = jnp.where(zl == 0, 2 * x + 2, 2 * x - 1)
    h_x_far = jnp.where(zl == 0, 2 * x - 1, 2 * x + 2)
    inner = [
        (first_frame, h_near),
        (second_frame, h_near),
        (first_frame, h_far),
        (second_frame, h_far),
    ]
    beside = [(b_frame, h_far), (b_frame, h_near)]
    near_ids = near_q[rows, :list_length].astype(jnp.int32)
    far_ids = far_q[rows, :list_length].astype(jnp.int32)
    near_listed = listed_slots(
        near_ids,
        inner + [(first_frame, h_x_far), (second_frame, h_x_far)] + beside + [(b_frame, h_x_far)],
        core,
    )
    far_listed = listed_slots(
        far_ids,
        inner + [(first_frame, h_x_near), (second_frame, h_x_near)] + beside + [(b_frame, h_x_near)],
        core,
    )

    near_stats, near_acc, far_stats, far_acc = block_attention(
        near_listed, far_listed, near_q, far_q, pair, far_pair
    )

    first_device = (flat((zh, core, x, zl)) == 0).astype(jnp.int32).reshape(1)
    text_acc, text_stats = text_partial(first_device, text, kv)
    devices = lax.axis_size(AX)
    share = text_acc.shape[1] // devices
    parts = jnp.concatenate(
        [
            jnp.transpose(text_acc.reshape(heads, devices, share, HD), (1, 0, 2, 3)).reshape(
                devices, heads * share, HD
            ),
            text_stats.reshape(devices, share, HD),
        ],
        axis=1,
    )
    merged = merge_text(lax.all_to_all(parts, AX, 0, 0), heads, share)
    text_out = spread(merged.astype(jnp.bfloat16), AX).reshape(text_acc.shape[1], columns)

    far_out = rest_attention(
        far_listed, far_q, x_near, [b_far, b_near, x_b_near], text, far_stats, far_acc, "rest_far"
    )
    back_first = lax.ppermute(far_out, AX, OUT_FAR_FIRST)
    back_second = lax.ppermute(far_out, AX, OUT_FAR_SECOND)
    near_out = rest_attention(
        near_listed, near_q, x_far, [b_far, b_near, x_b_far], text, near_stats, near_acc, "rest_near"
    )
    back_near = lax.ppermute(near_out, AX, OUT_NEAR)
    mine = jnp.where(straight, near_out, back_second)
    theirs = jnp.where(straight, back_near, back_first)
    latent_out = jnp.stack(
        [jnp.where(zl == 0, mine, theirs), jnp.where(zl == 0, theirs, mine)]
    )
    return (latent_out[None, None], text_out)


def solution(mesh):
    frames, heights, head = mesh.axis_names
    split = Mesh(
        mesh.devices.reshape(SIZES + (mesh.shape[head],)), AX + (head,)
    )
    tm, height = (("zh", "core"), ("x", "zl"))
    placed = (
        P(tm, height, None, None, head),
        P(None, tm, height, None, None, head),
        P(None, tm + height, None, head),
        P(tm, height, None, None),
        P(head),
    )
    return jax.shard_map(
        body,
        mesh=split,
        in_specs=placed,
        out_specs=(P(tm, height, None, None, head), P(None, head)),
        check_vma=False,
    )
```
